32 devices in a mesh: tenant: 2 (over x), store: 16 (over z, y, core).
Axes of the slice: x: 2, y: 2, z: 4, core: 2. Of those that a mesh axis runs over, the one named last changes fastest.
Arguments:
- queries: bfloat16 [4096, 1024], P(('tenant', 'store')), parts along dimension 0, may hold values from -24 to 24
- own_kv: bfloat16 [4096, 256], P(('tenant', 'store')), parts along dimension 0, may hold values from -15 to 15
- store_kv: bfloat16 [1024, 256, 256], P(('tenant', 'store')), parts along dimension 0, may hold values from -15 to 15
- q_start: int32 [32], P(('tenant', 'store')), parts along dimension 0, may hold values from 12288 to 16255
- pop_ids: int32 [8], P('tenant'), parts along dimension 0, may hold values from 0 to 511
- pop_pos: int32 [32, 4], P(('tenant', 'store')), parts along dimension 0, may hold values from 0 to 12287
- rare_ids: int32 [32, 6], P(('tenant', 'store')), parts along dimension 0, may hold values from 0 to 511, as said below
- rare_count: int32 [32], P(('tenant', 'store')), parts along dimension 0, may hold values from 4 to 6, as said below
- rare_pos: int32 [32, 6], P(('tenant', 'store')), parts along dimension 0, may hold values from 0 to 12287
Outputs:
- attended: bfloat16 [4096, 1024], P(('tenant', 'store')), parts along dimension 0
The draws below stay inside these ranges and needn't reach their ends.
There are 2 independent parts, one for each index of `tenant`. The reference program is written for one: setup_inputs(seed, part) draws one part's arguments, and reference() takes and returns one part's arrays. A program takes and returns all parts, laid end to end along the dimension named above; each array names one. Nothing has to cross between parts.
Inputs may be any that keep to these rules, and one draw needn't show every extreme that they name: `rare_ids`: the first rare_count entries of one device's list name blocks of different holders (id // 32); entries after them are ignored. `rare_count`: some device requests exactly 6 blocks and another exactly 4.
All inputs are finite; a program needn't handle non-finite values.
Results may differ from the reference program's by a relative error of at most 0.0085.
The reference program's roundings to bfloat16 on the way count: a program that leaves them out, or rounds other values in their place, can miss the bound.
Values may be sent and summed in bfloat16 or wider, within the bound.
A program may use at most 128 MiB of HBM per device.

```python
import jax
import jax.numpy as jnp
from jax import lax

HD = 128
GROUP = 8
QT = 128
SPAN = 256
CH_DEV = 32
POP = 4
TOKENS = 2048
SPANS = 512
RMAX = 6
RMIN = 4
N_STORE = 16


def shared_direction(key):
    pair_count = max(1, min(4, HD // 16))
    feature = jnp.arange(HD, dtype=jnp.int32)
    chosen = feature % (HD // 2) >= HD // 2 - pair_count
    signs = 2.0 * jax.random.randint(jax.random.fold_in(key, 21), (HD,), 0, 2).astype(jnp.float32) - 1.0
    return jnp.where(chosen, signs, 0.0)


def shape_keys(key, raw, salt):
    direction = shared_direction(key)
    lead_shape = raw.shape[:-1]
    picked = jax.random.randint(jax.random.fold_in(key, salt + 7), lead_shape, 0, 32) == 0
    key_part = raw[..., :HD]
    value_part = raw[..., HD:]
    key_part = jnp.where(picked[..., None], 0.2 * key_part + 3.6 * direction, key_part)
    return jnp.clip(jnp.concatenate([key_part, value_part], axis=-1), -15.0, 15.0).astype(jnp.bfloat16)


def draw_queries(key, part):
    direction = jnp.tile(shared_direction(key), GROUP)
    base = jax.random.normal(key, (TOKENS, GROUP * HD), jnp.float32)
    base = base + 3.0 * direction[None, :]
    return jnp.clip(base, -24.0, 24.0).astype(jnp.bfloat16)


def draw_own_kv(key, part):
    main_key = jax.random.fold_in(key, 42)
    raw = 2.5 * jax.random.normal(main_key, (TOKENS, 2 * HD), jnp.float32)
    return shape_keys(key, raw, 42)


def draw_store_kv(key, part):
    main_key = jax.random.fold_in(key, 41)
    raw = 2.5 * jax.random.normal(main_key, (SPANS, SPAN, 2 * HD), jnp.float32)
    return shape_keys(key, raw, 41)


def rare_tables(key):
    key_hot = jax.random.fold_in(key, 11)
    key_noise = jax.random.fold_in(key, 12)
    key_slot = jax.random.fold_in(key, 13)
    key_count = jax.random.fold_in(key, 14)
    key_peak = jax.random.fold_in(key, 15)
    hot_order = jax.random.permutation(key_hot, N_STORE)
    bias = jnp.where(hot_order < 4, 1 << 22, 0).astype(jnp.int32)
    noise = jax.random.randint(key_noise, (N_STORE, N_STORE), 0, 1 << 20)
    score = (noise + bias[None, :]) * N_STORE + jnp.arange(N_STORE, dtype=jnp.int32)[None, :]
    ranked, holders = lax.top_k(score, RMAX)
    slot_pick = jax.random.randint(key_slot, (N_STORE, RMAX), 0, CH_DEV)
    block_ids = holders.astype(jnp.int32) * CH_DEV + slot_pick
    counts = jax.random.randint(key_count, (N_STORE,), RMIN, RMAX + 1)
    peak_dev = jax.random.randint(key_peak, (), 0, N_STORE)
    device_index = jnp.arange(N_STORE, dtype=jnp.int32)
    counts = jnp.where(device_index == peak_dev, RMAX, counts)
    counts = jnp.where(device_index == (peak_dev + 1) % N_STORE, RMIN, counts)
    return (block_ids.astype(jnp.int32), counts.astype(jnp.int32))


def draw_rare_ids(key, part):
    block_ids, counts = rare_tables(key)
    return block_ids


def draw_rare_count(key, part):
    block_ids, counts = rare_tables(key)
    return counts


def place_ends(drawn, key, smallest, largest):
    index_at = [jax.random.randint(jax.random.fold_in(key, axis), (), 0, length) for axis, length in enumerate(drawn.shape)]
    main_axis = drawn.shape.index(max(drawn.shape))
    neighbour = index_at[:main_axis] + [(index_at[main_axis] + 1) % drawn.shape[main_axis]] + index_at[main_axis + 1:]
    return drawn.at[tuple(index_at)].set(smallest).at[tuple(neighbour)].set(largest)


def setup_inputs(seed: int = 0, part: int = 0) -> dict:
    key_list = jax.random.split(jax.random.key(seed), 10)
    part_keys = jax.random.split(jax.random.fold_in(key_list[9], part), 10)
    return {
        "queries": draw_queries(jax.random.fold_in(jax.random.fold_in(key_list[9], part), 71), part),
        "own_kv": draw_own_kv(jax.random.fold_in(jax.random.fold_in(key_list[9], part), 71), part),
        "store_kv": draw_store_kv(jax.random.fold_in(jax.random.fold_in(key_list[9], part), 71), part),
        "q_start": place_ends(jax.random.randint(part_keys[3], (N_STORE,), 12288, 16384 - QT), jax.random.fold_in(part_keys[3], 1), 12288, (16384 - QT) - 1).astype(jnp.int32),
        "pop_ids": place_ends(jax.random.randint(part_keys[4], (POP,), 0, SPANS), jax.random.fold_in(part_keys[4], 1), 0, SPANS - 1).astype(jnp.int32),
        "pop_pos": place_ends(jax.random.randint(part_keys[5], (N_STORE, POP), 0, 12288), jax.random.fold_in(part_keys[5], 1), 0, 12287).astype(jnp.int32),
        "rare_ids": draw_rare_ids(jax.random.fold_in(jax.random.fold_in(key_list[9], part), 71), part),
        "rare_count": draw_rare_count(jax.random.fold_in(jax.random.fold_in(key_list[9], part), 71), part),
        "rare_pos": place_ends(jax.random.randint(part_keys[8], (N_STORE, RMAX), 0, 12288), jax.random.fold_in(part_keys[8], 1), 0, 12287).astype(jnp.int32),
    }


def rotate(values, positions, head_size):
    half_size = head_size // 2
    freq_table = 500000.0 ** (-(2.0 * jnp.arange(half_size, dtype=jnp.float32)) / head_size)
    angles = positions.astype(jnp.float32)[:, None] * freq_table[None, :]
    cosine = jnp.cos(angles)[:, None, :]
    sine_part = jnp.sin(angles)[:, None, :]
    shaped = values.reshape(values.shape[0], -1, 2, half_size)
    first_half = shaped[:, :, 0, :]
    second_half = shaped[:, :, 1, :]
    turned = jnp.stack([first_half * cosine - second_half * sine_part, second_half * cosine + first_half * sine_part], axis=2)
    return turned.reshape(values.shape)


def block_stats(query_rows, key_rows, value_rows, allowed, scale_factor):
    scores = jnp.dot(query_rows, key_rows.T, preferred_element_type=jnp.float32) * scale_factor
    scores = jnp.where(allowed, scores, -jnp.inf)
    top_score = jnp.max(scores, axis=1)
    weights = jnp.exp(scores - top_score[:, None]).astype(jnp.bfloat16)
    weight_sum = jnp.sum(weights.astype(jnp.float32), axis=1)
    mixed_part = jnp.dot(weights, value_rows, preferred_element_type=jnp.float32)
    return top_score, weight_sum, mixed_part


def reference(queries, own_kv, store_kv, q_start, pop_ids, pop_pos, rare_ids, rare_count, rare_pos):
    scale_factor = HD ** -0.5

    def one_device(inputs):
        query_block, own_block, start_pos, pop_offsets, rare_list, rare_total, rare_offsets = inputs
        positions = start_pos + jnp.arange(QT, dtype=jnp.int32)
        query_rows = rotate(query_block.astype(jnp.float32), positions, HD).astype(jnp.bfloat16).reshape(QT * GROUP, HD)
        own_keys = rotate(own_block[:, :HD].astype(jnp.float32), positions, HD).astype(jnp.bfloat16)
        causal = (jnp.arange(QT * GROUP) // GROUP)[:, None] >= jnp.arange(QT)[None, :]
        own_top, own_sum, own_mixed = block_stats(query_rows, own_keys, own_block[:, HD:], causal, scale_factor)
        span_list = jnp.concatenate([pop_ids, rare_list]).astype(jnp.int32)
        offsets = jnp.concatenate([pop_offsets, rare_offsets]).astype(jnp.int32)
        present = jnp.concatenate([jnp.ones((POP,), jnp.bool_), jnp.arange(RMAX) < rare_total])

        def span_stats(item):
            span_id, offset, is_present = item
            span_kv = lax.dynamic_index_in_dim(store_kv, span_id, 0, keepdims=False)
            span_keys = rotate(span_kv[:, :HD].astype(jnp.float32), offset + jnp.arange(SPAN, dtype=jnp.int32), HD).astype(jnp.bfloat16)
            top_score, weight_sum, mixed_part = block_stats(query_rows, span_keys, span_kv[:, HD:], True, scale_factor)
            return jnp.where(is_present, top_score, -jnp.inf), weight_sum, mixed_part

        tops, sums, mixes = lax.map(span_stats, (span_list, offsets, present))
        tops = jnp.concatenate([own_top[None], tops], axis=0)
        sums = jnp.concatenate([own_sum[None], sums], axis=0)
        mixes = jnp.concatenate([own_mixed[None], mixes], axis=0)
        peak = jnp.max(tops, axis=0)
        factor = jnp.exp(tops - peak[None, :])
        numer = jnp.sum(factor[:, :, None] * mixes, axis=0)
        denom = jnp.sum(factor * sums, axis=0)
        return (numer / denom[:, None]).reshape(QT, GROUP * HD).astype(jnp.bfloat16)

    result = lax.map(one_device, (queries.reshape(N_STORE, QT, GROUP * HD), own_kv.reshape(N_STORE, QT, 2 * HD), q_start, pop_pos, rare_ids, rare_count, rare_pos))
    return result.reshape(N_STORE * QT, GROUP * HD)
```

```python
import functools

import jax
import jax.numpy as jnp
import numpy as np
from jax import lax
from jax.experimental import pallas as pl
from jax.experimental.pallas import tpu as pltpu
from jax.sharding import PartitionSpec as P

MESH = pl.DeviceIdType.MESH
INNER = 4


def kernel(
    n, per_device, requests, pops, chunk, scale,
    table_ref, pop_ref, request_ref, queries_ref, own_ref, store_hbm,
    base_cos, base_sin, step_cos, step_sin, out_ref,
    store, asks, asks_s, stage, recv, query_rows, total, tops,
    one_stage, one_recv, two_stage, two_recv, three_stage, popular,
    local_sem, ask_send, ask_recv, rare_send, rare_recv,
    one_send, one_sem, two_send, two_sem, three_send, three_sem,
):
    me = lax.axis_index("store")
    inner, outer = lax.rem(me, INNER), me // INNER
    outers = n // INNER
    head = base_cos.shape[1]
    tokens = queries_ref.shape[0]
    rows = query_rows.shape[0]
    span = stage.shape[1]
    piece = span // INNER

    def ask_copy(slot, target):
        return pltpu.make_async_remote_copy(
            src_ref=request_ref, dst_ref=asks.at[slot],
            send_sem=ask_send.at[target], recv_sem=ask_recv.at[slot],
            device_id={"store": target}, device_id_type=MESH)

    def rare_copy(slot, target):
        return pltpu.make_async_remote_copy(
            src_ref=stage.at[target], dst_ref=recv.at[slot],
            send_sem=rare_send.at[target], recv_sem=rare_recv.at[slot],
            device_id={"store": target}, device_id_type=MESH)

    def one_copy(slot, target):
        return pltpu.make_async_remote_copy(
            src_ref=one_stage.at[target], dst_ref=one_recv.at[slot],
            send_sem=one_send.at[target], recv_sem=one_sem.at[slot],
            device_id={"store": outer * INNER + target}, device_id_type=MESH)

    def two_copy(slot, target):
        return pltpu.make_async_remote_copy(
            src_ref=two_stage, dst_ref=two_recv.at[slot],
            send_sem=two_send.at[target], recv_sem=two_sem.at[slot],
            device_id={"store": target * INNER + inner}, device_id_type=MESH)

    def three_copy(slot, target):
        return pltpu.make_async_remote_copy(
            src_ref=three_stage, dst_ref=popular.at[slot],
            send_sem=three_send.at[target], recv_sem=three_sem.at[slot],
            device_id={"store": outer * INNER + target}, device_id_type=MESH)

    def peers(act):
        def step(s, carry):
            act(lax.rem(me + s, n))
            return carry
        lax.fori_loop(1, n, step, 0)

    load = pltpu.make_async_copy(store_hbm, store, local_sem.at[0])
    load.start()
    barrier = pltpu.get_barrier_semaphore()
    peers(lambda d: pl.semaphore_signal(
        barrier, inc=1, device_id={"store": d}, device_id_type=MESH))
    pl.semaphore_wait(barrier, n - 1)
    peers(lambda d: ask_copy(me, d).start())
    load.wait()

    for s in range(INNER):
        j = lax.rem(inner + s, INNER)
        begin = pl.multiple_of(j * piece, piece)
        for k in range(pops):
            part = store[lax.rem(pop_ref[k], per_device), pl.ds(begin, piece), :]
            if s == 0:
                one_recv[inner, k] = part
            else:
                one_stage[j, k] = part
        if s:
            one_copy(inner, j).start()

    cos0, sin0 = base_cos[0:1, :], base_sin[0:1, :]
    cos_n, sin_n = step_cos[:tokens, :], step_sin[:tokens, :]
    own_cos = cos0 * cos_n - sin0 * sin_n
    own_sin = sin0 * cos_n + cos0 * sin_n

    def turn(x, cosine, sine):
        x = x.astype(jnp.float32)
        return (x * cosine + pltpu.roll(x, head // 2, 1) * sine).astype(jnp.bfloat16)

    for g in range(rows // tokens):
        query_rows[g * tokens:(g + 1) * tokens, :] = turn(
            queries_ref[:, g * head:(g + 1) * head], own_cos, own_sin)

    def scores_of(at, keys):
        return lax.dot_general(
            query_rows[at, :], keys, (((1,), (1,)), ((), ())),
            preferred_element_type=jnp.float32) * scale

    def fold(block, base, live):
        cos_b, sin_b = base_cos[pl.ds(base, 1), :], base_sin[pl.ds(base, 1), :]
        cos_n, sin_n = step_cos[:span, :], step_sin[:span, :]
        keys = turn(
            block[:, :head], cos_b * cos_n - sin_b * sin_n, sin_b * cos_n + cos_b * sin_n)
        values = jnp.concatenate(
            [block[:, head:], jnp.ones((span, head), jnp.bfloat16)], axis=1)
        for c in range(rows // chunk):
            at = pl.ds(c * chunk, chunk)
            scores = scores_of(at, keys)
            top = jnp.max(scores, axis=1, keepdims=True)
            weights = jnp.exp(scores - top).astype(jnp.bfloat16)
            mixed = jnp.dot(weights, values, preferred_element_type=jnp.float32)
            top = jnp.where(live, top, -jnp.inf)
            old = tops[at, :]
            diff = top - old
            factor = jnp.exp(-jnp.abs(diff))
            rises = diff > 0.0
            keep = jnp.where(rises, factor, 1.0)
            take = jnp.where(rises, 1.0, factor)
            tops[at, :] = jnp.maximum(old, top)
            total[at, :head] = total[at, :head] * keep + mixed[:, :head] * take
            total[at, head:] = total[at, head:] * keep + mixed[:, head:] * take

    peers(lambda d: ask_copy(d, d).wait_recv())
    bring = pltpu.make_async_copy(asks, asks_s, local_sem.at[1])
    asks[me] = request_ref[...]
    bring.start()
    bring.wait()

    def slot_for(d):
        def look(r, slot):
            block_id = asks_s[d, 0, r]
            hit = (block_id // per_device == me) & (r < asks_s[d, 0, requests])
            return jnp.where(hit, lax.rem(block_id, per_device), slot)
        return lax.fori_loop(0, requests, look, jnp.int32(0), unroll=min(requests, 8))

    for s in range(1, INNER):
        j = lax.rem(inner + s, INNER)
        one_copy(j, j).wait_recv()
    for k in range(pops):
        holder = pop_ref[k] // per_device
        two_stage[k] = one_recv[lax.rem(holder, INNER), k]

    def two_start(s, carry):
        two_copy(outer, lax.rem(outer + s, outers)).start()
        return carry
    lax.fori_loop(1, outers, two_start, 0)
    two_recv[outer] = two_stage[...]

    def reply(d):
        stage[d] = store[slot_for(d)]
        rare_copy(me, d).start()
    peers(reply)
    recv[me] = store[slot_for(me)]

    own_keys = turn(own_ref[:, :head], own_cos, own_sin)
    own_values = jnp.concatenate(
        [own_ref[:, head:], jnp.ones((tokens, head), jnp.bfloat16)], axis=1)
    for c in range(rows // chunk):
        at = pl.ds(c * chunk, chunk)
        token = lax.rem(
            lax.broadcasted_iota(jnp.int32, (chunk, tokens), 0) + c * chunk, tokens)
        seen = token >= lax.broadcasted_iota(jnp.int32, (chunk, tokens), 1)
        scores = jnp.where(seen, scores_of(at, own_keys), -jnp.inf)
        top = jnp.max(scores, axis=1, keepdims=True)
        weights = jnp.exp(scores - top).astype(jnp.bfloat16)
        total[at, :] = jnp.dot(weights, own_values, preferred_element_type=jnp.float32)
        tops[at, :] = top

    def two_wait(s, carry):
        d = lax.rem(outer + s, outers)
        two_copy(d, d).wait_recv()
        return carry
    lax.fori_loop(1, outers, two_wait, 0)
    for k in range(pops):
        three_stage[k] = two_recv[pop_ref[k] // (per_device * INNER), k]
    for s in range(1, INNER):
        three_copy(inner, lax.rem(inner + s, INNER)).start()
    popular[inner] = three_stage[...]

    def rare_fold(h):
        def look(r, found):
            hit = (table_ref[r] // per_device == h) & (r < table_ref[requests])
            return jnp.where(hit, r, found)
        r = lax.fori_loop(0, requests, look, jnp.int32(-1), unroll=min(requests, 8))
        fold(recv[h], jnp.maximum(r, 0) + 1 + pops, r >= 0)

    def arrival(s, carry):
        h = lax.rem(me + n - s, n)

        @pl.when(s > 0)
        def _():
            rare_copy(h, h).wait_recv()
        rare_fold(h)
        return carry
    early = min(n, 4)
    lax.fori_loop(0, early, arrival, 0)

    for s in range(1, INNER):
        j = lax.rem(inner + s, INNER)
        three_copy(j, j).wait_recv()

    def popular_fold(k, carry):
        block = jnp.concatenate([popular[j, k] for j in range(INNER)], axis=0)
        fold(block, k + 1, True)
        return carry
    lax.fori_loop(0, pops, popular_fold, 0)
    lax.fori_loop(early, n, arrival, 0)

    for g in range(rows // tokens):
        at = pl.ds(g * tokens, tokens)
        out_ref[:, g * head:(g + 1) * head] = (
            total[at, :head] / total[at, head:]).astype(jnp.bfloat16)

    peers(lambda d: ask_copy(d, d).wait_send())
    peers(lambda d: rare_copy(d, d).wait_send())
    for s in range(1, INNER):
        j = lax.rem(inner + s, INNER)
        one_copy(j, j).wait_send()
        three_copy(j, j).wait_send()

    def two_done(s, carry):
        d = lax.rem(outer + s, outers)
        two_copy(d, d).wait_send()
        return carry
    lax.fori_loop(1, outers, two_done, 0)


def body(queries, own_kv, store_kv, q_start, pop_ids, pop_pos, rare_ids, rare_count, rare_pos):
    n = lax.axis_size("store")
    tokens = queries.shape[0]
    head = own_kv.shape[1] // 2
    rows = tokens * (queries.shape[1] // head)
    per_device, span, width = store_kv.shape
    requests = rare_ids.shape[1]
    pops = pop_ids.shape[0]
    longest = max(span, tokens)
    lanes = -(-(requests + 1) // 128) * 128
    outers = n // INNER
    piece = span // INNER

    half = np.arange(head) % (head // 2)
    freq = 500000.0 ** (-(2.0 * half) / head)
    sign = np.where(np.arange(head) < head // 2, -1.0, 1.0)
    steps = np.arange(longest)[:, None] * freq[None, :]
    step_cos = np.cos(steps).astype(np.float32)
    step_sin = (np.sin(steps) * sign).astype(np.float32)
    base = jnp.concatenate([q_start, pop_pos[0], rare_pos[0]]).astype(jnp.float32)
    angles = base[:, None] * freq.astype(np.float32)[None, :]
    base_cos = jnp.cos(angles)
    base_sin = jnp.sin(angles) * sign.astype(np.float32)[None, :]
    table = jnp.concatenate([rare_ids[0], rare_count])
    table = jnp.pad(table, (0, lanes - requests - 1))

    vmem = pl.BlockSpec(memory_space=pltpu.VMEM)
    smem = pl.BlockSpec(memory_space=pltpu.SMEM)
    dma = pltpu.SemaphoreType.DMA
    bf16 = jnp.bfloat16
    chunk = min(rows, 256)
    return pl.pallas_call(
        functools.partial(kernel, n, per_device, requests, pops, chunk, head ** -0.5),
        out_shape=jax.ShapeDtypeStruct(queries.shape, bf16),
        in_specs=[smem, smem, vmem, vmem, vmem, pl.BlockSpec(memory_space=pl.ANY)] + [vmem] * 4,
        out_specs=vmem,
        scratch_shapes=[
            pltpu.VMEM((per_device, span, width), bf16),
            pltpu.VMEM((n, 1, lanes), jnp.int32),
            pltpu.SMEM((n, 1, lanes), jnp.int32),
            pltpu.VMEM((n, span, width), bf16),
            pltpu.VMEM((n, span, width), bf16),
            pltpu.VMEM((rows, head), bf16),
            pltpu.VMEM((rows, 2 * head), jnp.float32),
            pltpu.VMEM((rows, 1), jnp.float32),
            pltpu.VMEM((INNER, pops, piece, width), bf16),
            pltpu.VMEM((INNER, pops, piece, width), bf16),
            pltpu.VMEM((pops, piece, width), bf16),
            pltpu.VMEM((outers, pops, piece, width), bf16),
            pltpu.VMEM((pops, piece, width), bf16),
            pltpu.VMEM((INNER, pops, piece, width), bf16),
            dma((2,)), dma((n,)), dma((n,)), dma((n,)), dma((n,)),
            dma((INNER,)), dma((INNER,)), dma((outers,)), dma((outers,)),
            dma((INNER,)), dma((INNER,)),
        ],
        compiler_params=pltpu.CompilerParams(
            collective_id=0, has_side_effects=True, vmem_limit_bytes=60 * 2**20),
    )(table, pop_ids, table.reshape(1, lanes), queries, own_kv, store_kv,
      base_cos, base_sin, step_cos, step_sin)


def solution(mesh):
    both = ("tenant", "store")
    in_specs = (
        P(both, None), P(both, None), P(both, None, None), P(both), P("tenant"),
        P(both, None), P(both, None), P(both), P(both, None),
    )
    return jax.shard_map(
        body, mesh=mesh, in_specs=in_specs, out_specs=P(both, None), check_vma=False)
```

```python
import functools

import jax
import jax.numpy as jnp
import numpy as np
from jax import lax
from jax.experimental import pallas as pl
from jax.experimental.pallas import tpu as pltpu
from jax.sharding import PartitionSpec as P

MESH = pl.DeviceIdType.MESH
INNER = 4


def kernel(
    n, per_device, requests, pops, chunk, power,
    table_ref, pop_ref, request_ref, queries_ref, own_ref, store_hbm,
    base_cos, base_sin, step_cos, step_sin, out_ref,
    store, asks, asks_s, stage, recv, query_rows, total, tops,
    one_stage, one_recv, two_stage, two_recv, mid_stage, three_stage, popular,
    local_sem, ask_send, ask_recv, rare_send, rare_recv,
    one_send, one_sem, two_send, two_sem, mid_send, mid_sem, three_send, three_sem,
):
    me = lax.axis_index("store")
    inner, outer = lax.rem(me, INNER), me // INNER
    outers = n // INNER
    head = base_cos.shape[1]
    tokens = queries_ref.shape[0]
    rows = query_rows.shape[0]
    span = stage.shape[1]
    piece = span // INNER

    def ask_copy(slot, target):
        return pltpu.make_async_remote_copy(
            src_ref=request_ref, dst_ref=asks.at[slot],
            send_sem=ask_send.at[target], recv_sem=ask_recv.at[slot],
            device_id={"store": target}, device_id_type=MESH)

    def rare_copy(slot, target):
        return pltpu.make_async_remote_copy(
            src_ref=stage.at[target], dst_ref=recv.at[slot],
            send_sem=rare_send.at[target], recv_sem=rare_recv.at[slot],
            device_id={"store": target}, device_id_type=MESH)

    def one_copy(slot, target):
        return pltpu.make_async_remote_copy(
            src_ref=one_stage.at[target], dst_ref=one_recv.at[slot],
            send_sem=one_send.at[target], recv_sem=one_sem.at[slot],
            device_id={"store": outer * INNER + target}, device_id_type=MESH)

    def two_copy(slot, target):
        return pltpu.make_async_remote_copy(
            src_ref=two_stage.at[target], dst_ref=two_recv.at[slot],
            send_sem=two_send.at[target], recv_sem=two_sem.at[slot],
            device_id={"store": target * INNER + inner}, device_id_type=MESH)

    def mid_copy(slot, target):
        return pltpu.make_async_remote_copy(
            src_ref=mid_stage, dst_ref=three_stage.at[slot],
            send_sem=mid_send.at[target], recv_sem=mid_sem.at[slot],
            device_id={"store": target * INNER + inner}, device_id_type=MESH)

    def three_copy(slot, target):
        return pltpu.make_async_remote_copy(
            src_ref=three_stage, dst_ref=popular.at[slot],
            send_sem=three_send.at[target], recv_sem=three_sem.at[slot],
            device_id={"store": outer * INNER + target}, device_id_type=MESH)

    def peers(act):
        def step(s, carry):
            act(lax.rem(me + s, n))
            return carry
        lax.fori_loop(1, n, step, 0)

    load = pltpu.make_async_copy(store_hbm, store, local_sem.at[0])
    load.start()
    barrier = pltpu.get_barrier_semaphore()
    peers(lambda d: pl.semaphore_signal(
        barrier, inc=1, device_id={"store": d}, device_id_type=MESH))
    pl.semaphore_wait(barrier, n - 1)
    peers(lambda d: ask_copy(me, d).start())
    load.wait()

    for s in range(INNER):
        j = lax.rem(inner + s, INNER)
        begin = pl.multiple_of(j * piece, piece)
        for k in range(pops):
            part = store[lax.rem(pop_ref[k], per_device), pl.ds(begin, piece), :]
            if s == 0:
                one_recv[inner, k] = part
            else:
                one_stage[j, k] = part
        if s:
            one_copy(inner, j).start()

    cos0, sin0 = base_cos[0:1, :], base_sin[0:1, :]
    cos_n, sin_n = step_cos[:tokens, :], step_sin[:tokens, :]
    own_cos = cos0 * cos_n - sin0 * sin_n
    own_sin = sin0 * cos_n + cos0 * sin_n

    def turn(x, cosine, sine):
        x = x.astype(jnp.float32)
        return (x * cosine + pltpu.roll(x, head // 2, 1) * sine).astype(jnp.bfloat16)

    for g in range(rows // tokens):
        query_rows[g * tokens:(g + 1) * tokens, :] = turn(
            queries_ref[:, g * head:(g + 1) * head], own_cos, own_sin)

    pad = total.shape[0] - head

    def attend(keys, values, c, seen):
        at = pl.ds(c * chunk, chunk)
        scores = lax.dot_general(
            keys, query_rows[at, :], (((1,), (1,)), ((), ())),
            preferred_element_type=jnp.float32)
        if seen is not None:
            scores = jnp.where(seen, scores, -jnp.inf)
        top = jnp.max(scores, axis=0, keepdims=True)
        weights = jnp.exp2((scores - top) * power).astype(jnp.bfloat16)
        return top, jnp.dot(values, weights, preferred_element_type=jnp.float32)

    def flip(values):
        return jnp.concatenate(
            [values.T, jnp.ones((pad, values.shape[0]), jnp.bfloat16)], axis=0)

    def fold(block, base, live):
        cos_b, sin_b = base_cos[pl.ds(base, 1), :], base_sin[pl.ds(base, 1), :]
        cos_n, sin_n = step_cos[:span, :], step_sin[:span, :]
        keys = turn(
            block[:, :head], cos_b * cos_n - sin_b * sin_n, sin_b * cos_n + cos_b * sin_n)
        values = flip(block[:, head:])
        for c in range(rows // chunk):
            at = pl.ds(c * chunk, chunk)
            top, mixed = attend(keys, values, c, None)
            top = jnp.where(live, top, -jnp.inf)
            old = tops[:, at]
            diff = top - old
            factor = jnp.exp2(-jnp.abs(diff) * power)
            rises = diff > 0.0
            tops[:, at] = jnp.maximum(old, top)
            total[:, at] = (
                total[:, at] * jnp.where(rises, factor, 1.0)
                + mixed * jnp.where(rises, 1.0, factor))

    peers(lambda d: ask_copy(d, d).wait_recv())
    bring = pltpu.make_async_copy(asks, asks_s, local_sem.at[1])
    asks[me] = request_ref[...]
    bring.start()
    bring.wait()

    def slot_for(d):
        def look(r, slot):
            block_id = asks_s[d, 0, r]
            hit = (block_id // per_device == me) & (r < asks_s[d, 0, requests])
            return jnp.where(hit, lax.rem(block_id, per_device), slot)
        return lax.fori_loop(0, requests, look, jnp.int32(0), unroll=min(requests, 8))

    def reply(first, last):
        def step(s, carry):
            d = lax.rem(me + s, n)
            stage[d] = store[slot_for(d)]
            rare_copy(me, d).start()
            return carry
        lax.fori_loop(first, last, step, 0)

    cuts = [1, 3, 5, 7, n]
    reply(cuts[0], cuts[1])
    recv[me] = store[slot_for(me)]

    for s in range(1, INNER):
        j = lax.rem(inner + s, INNER)
        one_copy(j, j).wait_recv()
    for k in range(pops):
        two_stage[k] = one_recv[lax.rem(pop_ref[k] // per_device, INNER), k]
    for k in range(pops):
        @pl.when(outer != k)
        def _():
            two_copy(outer, k).start()

        @pl.when(outer == k)
        def _():
            two_recv[k] = two_stage[k]

    def rare_fold(h):
        def look(r, found):
            hit = (table_ref[r] // per_device == h) & (r < table_ref[requests])
            return jnp.where(hit, r, found)
        r = lax.fori_loop(0, requests, look, jnp.int32(-1), unroll=min(requests, 8))
        fold(recv[h], jnp.maximum(r, 0) + 1 + pops, r >= 0)

    def arrivals(first, last):
        def step(s, carry):
            h = lax.rem(me + n - s, n)
            rare_copy(h, h).wait_recv()
            rare_fold(h)
            return carry
        lax.fori_loop(first, last, step, 0)

    reply(cuts[1], cuts[2])

    own_keys = turn(own_ref[:, :head], own_cos, own_sin)
    own_values = flip(own_ref[:, head:])
    for c in range(rows // chunk):
        at = pl.ds(c * chunk, chunk)
        token = lax.rem(
            lax.broadcasted_iota(jnp.int32, (tokens, chunk), 1) + c * chunk, tokens)
        seen = token >= lax.broadcasted_iota(jnp.int32, (tokens, chunk), 0)
        top, total[:, at] = attend(own_keys, own_values, c, seen)
        tops[:, at] = top

    rare_fold(me)

    @pl.when(outer < pops)
    def _():
        def two_wait(s, carry):
            d = lax.rem(outer + s, outers)
            pltpu.make_async_remote_copy(
                src_ref=mid_stage, dst_ref=two_recv.at[d],
                send_sem=mid_send.at[d], recv_sem=two_sem.at[d],
                device_id={"store": d * INNER + inner}, device_id_type=MESH).wait_recv()
            return carry
        lax.fori_loop(1, outers, two_wait, 0)
        mine = lax.rem(outer, pops)
        mid_stage[...] = two_recv[pop_ref[mine] // (per_device * INNER)]

        def mid_start(s, carry):
            mid_copy(mine, lax.rem(outer + s, outers)).start()
            return carry
        lax.fori_loop(1, outers, mid_start, 0)
        three_stage[mine] = mid_stage[...]

    reply(cuts[2], cuts[3])
    arrivals(cuts[0], cuts[1])
    for k in range(pops):
        @pl.when(outer != k)
        def _():
            mid_copy(k, k).wait_recv()
    for s in range(1, INNER):
        three_copy(inner, lax.rem(inner + s, INNER)).start()
    for k in range(pops):
        popular[inner, k] = three_stage[k]
    reply(cuts[3], cuts[4])
    arrivals(cuts[1], cuts[3])

    for s in range(1, INNER):
        j = lax.rem(inner + s, INNER)
        three_copy(j, j).wait_recv()

    def popular_fold(k, carry):
        block = jnp.concatenate([popular[j, k] for j in range(INNER)], axis=0)
        fold(block, k + 1, True)
        return carry
    lax.fori_loop(0, pops, popular_fold, 0)

    arrivals(cuts[3], cuts[4])

    for g in range(rows // tokens):
        at = pl.ds(g * tokens, tokens)
        out_ref[:, g * head:(g + 1) * head] = (
            total[:head, at] / total[head:head + 1, at]).T.astype(jnp.bfloat16)

    peers(lambda d: ask_copy(d, d).wait_send())
    peers(lambda d: rare_copy(d, d).wait_send())
    for s in range(1, INNER):
        j = lax.rem(inner + s, INNER)
        one_copy(j, j).wait_send()
        three_copy(j, j).wait_send()

    for k in range(pops):
        @pl.when(outer != k)
        def _():
            two_copy(k, k).wait_send()

    @pl.when(outer < pops)
    def _():
        def mid_done(s, carry):
            d = lax.rem(outer + s, outers)
            mid_copy(lax.rem(outer, pops), d).wait_send()
            return carry
        lax.fori_loop(1, outers, mid_done, 0)


def body(queries, own_kv, store_kv, q_start, pop_ids, pop_pos, rare_ids, rare_count, rare_pos):
    n = lax.axis_size("store")
    tokens = queries.shape[0]
    head = own_kv.shape[1] // 2
    rows = tokens * (queries.shape[1] // head)
    per_device, span, width = store_kv.shape
    requests = rare_ids.shape[1]
    pops = pop_ids.shape[0]
    longest = max(span, tokens)
    lanes = -(-(requests + 1) // 128) * 128
    outers = n // INNER
    piece = span // INNER

    half = np.arange(head) % (head // 2)
    freq = 500000.0 ** (-(2.0 * half) / head)
    sign = np.where(np.arange(head) < head // 2, -1.0, 1.0)
    steps = np.arange(longest)[:, None] * freq[None, :]
    step_cos = np.cos(steps).astype(np.float32)
    step_sin = (np.sin(steps) * sign).astype(np.float32)
    base = jnp.concatenate([q_start, pop_pos[0], rare_pos[0]]).astype(jnp.float32)
    angles = base[:, None] * freq.astype(np.float32)[None, :]
    base_cos = jnp.cos(angles)
    base_sin = jnp.sin(angles) * sign.astype(np.float32)[None, :]
    table = jnp.concatenate([rare_ids[0], rare_count])
    table = jnp.pad(table, (0, lanes - requests - 1))

    vmem = pl.BlockSpec(memory_space=pltpu.VMEM)
    smem = pl.BlockSpec(memory_space=pltpu.SMEM)
    dma = pltpu.SemaphoreType.DMA
    bf16 = jnp.bfloat16
    chunk = min(rows, 256)
    return pl.pallas_call(
        functools.partial(kernel, n, per_device, requests, pops, chunk, head ** -0.5 * np.log2(np.e).item()),
        out_shape=jax.ShapeDtypeStruct(queries.shape, bf16),
        in_specs=[smem, smem, vmem, vmem, vmem, pl.BlockSpec(memory_space=pl.ANY)] + [vmem] * 4,
        out_specs=vmem,
        scratch_shapes=[
            pltpu.VMEM((per_device, span, width), bf16),
            pltpu.VMEM((n, 1, lanes), jnp.int32),
            pltpu.SMEM((n, 1, lanes), jnp.int32),
            pltpu.VMEM((n, span, width), bf16),
            pltpu.VMEM((n, span, width), bf16),
            pltpu.VMEM((rows, head), bf16),
            pltpu.VMEM((head + 16, rows), jnp.float32),
            pltpu.VMEM((1, rows), jnp.float32),
            pltpu.VMEM((INNER, pops, piece, width), bf16),
            pltpu.VMEM((INNER, pops, piece, width), bf16),
            pltpu.VMEM((pops, piece, width), bf16),
            pltpu.VMEM((outers, piece, width), bf16),
            pltpu.VMEM((piece, width), bf16),
            pltpu.VMEM((pops, piece, width), bf16),
            pltpu.VMEM((INNER, pops, piece, width), bf16),
            dma((2,)), dma((n,)), dma((n,)), dma((n,)), dma((n,)),
            dma((INNER,)), dma((INNER,)), dma((outers,)), dma((outers,)), dma((outers,)), dma((pops,)),
            dma((INNER,)), dma((INNER,)),
        ],
        compiler_params=pltpu.CompilerParams(
            collective_id=0, has_side_effects=True, vmem_limit_bytes=60 * 2**20),
    )(table, pop_ids, table.reshape(1, lanes), queries, own_kv, store_kv,
      base_cos, base_sin, step_cos, step_sin)


def solution(mesh):
    both = ("tenant", "store")
    in_specs = (
        P(both, None), P(both, None), P(both, None, None), P(both), P("tenant"),
        P(both, None), P(both, None), P(both), P(both, None),
    )
    return jax.shard_map(
        body, mesh=mesh, in_specs=in_specs, out_specs=P(both, None), check_vma=False)
```

```python
import functools

import jax
import jax.numpy as jnp
import numpy as np
from jax import lax
from jax.experimental import pallas as pl
from jax.experimental.pallas import tpu as pltpu
from jax.sharding import PartitionSpec as P

MESH = pl.DeviceIdType.MESH
INNER = 4
STRIDE = 5
WINDOW = 6


def kernel(
    n, per_device, requests, pops, chunk, power,
    pop_ref, request_ref, queries_ref, own_ref, store_hbm,
    base_cos, base_sin, step_cos, step_sin, out_ref,
    store, asks, asks_s, stage, recv, query_rows, total, tops,
    one_stage, one_recv, two_stage, two_recv, mid_stage, three_stage, popular,
    local_sem, ask_send, ask_recv, rare_send, rare_recv,
    one_send, one_sem, two_send, two_sem, mid_send, mid_sem, three_send, three_sem,
):
    me = lax.axis_index("store")
    inner, outer = lax.rem(me, INNER), me // INNER
    outers = n // INNER
    head = base_cos.shape[1]
    tokens = queries_ref.shape[0]
    rows = query_rows.shape[0]
    span = stage.shape[1]
    piece = span // INNER

    def ask_copy(slot, target):
        return pltpu.make_async_remote_copy(
            src_ref=request_ref, dst_ref=asks.at[slot],
            send_sem=ask_send.at[target], recv_sem=ask_recv.at[slot],
            device_id={"store": target}, device_id_type=MESH)

    def rare_copy(slot, target):
        return pltpu.make_async_remote_copy(
            src_ref=stage.at[target], dst_ref=recv.at[slot],
            send_sem=rare_send.at[target], recv_sem=rare_recv.at[slot],
            device_id={"store": target}, device_id_type=MESH)

    def one_copy(slot, target):
        return pltpu.make_async_remote_copy(
            src_ref=one_stage.at[target], dst_ref=one_recv.at[slot],
            send_sem=one_send.at[target], recv_sem=one_sem.at[slot],
            device_id={"store": outer * INNER + target}, device_id_type=MESH)

    def two_copy(slot, target):
        return pltpu.make_async_remote_copy(
            src_ref=two_stage.at[target], dst_ref=two_recv.at[slot],
            send_sem=two_send.at[target], recv_sem=two_sem.at[slot],
            device_id={"store": target * INNER + inner}, device_id_type=MESH)

    def mid_copy(slot, target):
        return pltpu.make_async_remote_copy(
            src_ref=mid_stage, dst_ref=three_stage.at[slot],
            send_sem=mid_send.at[target], recv_sem=mid_sem.at[slot],
            device_id={"store": target * INNER + inner}, device_id_type=MESH)

    def three_copy(slot, target):
        return pltpu.make_async_remote_copy(
            src_ref=three_stage, dst_ref=popular.at[slot],
            send_sem=three_send.at[target], recv_sem=three_sem.at[slot],
            device_id={"store": outer * INNER + target}, device_id_type=MESH)

    def peers(act):
        def step(s, carry):
            act(lax.rem(me + s, n))
            return carry
        lax.fori_loop(1, n, step, 0)

    load = pltpu.make_async_copy(store_hbm, store, local_sem.at[0])
    load.start()
    barrier = pltpu.get_barrier_semaphore()
    peers(lambda d: pl.semaphore_signal(
        barrier, inc=1, device_id={"store": d}, device_id_type=MESH))
    pl.semaphore_wait(barrier, n - 1)
    peers(lambda d: ask_copy(me, d).start())
    load.wait()

    for s in range(INNER):
        j = lax.rem(inner + s, INNER)
        begin = pl.multiple_of(j * piece, piece)
        for k in range(pops):
            part = store[lax.rem(pop_ref[k], per_device), pl.ds(begin, piece), :]
            if s == 0:
                one_recv[inner, k] = part
            else:
                one_stage[j, k] = part
        if s:
            one_copy(inner, j).start()

    cos0, sin0 = base_cos[0:1, :], base_sin[0:1, :]
    cos_n, sin_n = step_cos[:tokens, :], step_sin[:tokens, :]
    own_cos = cos0 * cos_n - sin0 * sin_n
    own_sin = sin0 * cos_n + cos0 * sin_n

    def turn(x, cosine, sine):
        x = x.astype(jnp.float32)
        return (x * cosine + pltpu.roll(x, head // 2, 1) * sine).astype(jnp.bfloat16)

    for g in range(rows // tokens):
        query_rows[g * tokens:(g + 1) * tokens, :] = turn(
            queries_ref[:, g * head:(g + 1) * head], own_cos, own_sin)

    pad = total.shape[0] - head

    def attend(keys, values, c, seen):
        at = pl.ds(c * chunk, chunk)
        scores = lax.dot_general(
            keys, query_rows[at, :], (((1,), (1,)), ((), ())),
            preferred_element_type=jnp.float32)
        if seen is not None:
            scores = jnp.where(seen, scores, -jnp.inf)
        top = jnp.max(scores, axis=0, keepdims=True)
        weights = jnp.exp2((scores - top) * power).astype(jnp.bfloat16)
        return top, jnp.dot(values, weights, preferred_element_type=jnp.float32)

    def flip(values):
        return jnp.concatenate(
            [values.T, jnp.ones((pad, values.shape[0]), jnp.bfloat16)], axis=0)

    def fold(block, base, live):
        cos_b, sin_b = base_cos[pl.ds(base, 1), :], base_sin[pl.ds(base, 1), :]
        cos_n, sin_n = step_cos[:span, :], step_sin[:span, :]
        keys = turn(
            block[:, :head], cos_b * cos_n - sin_b * sin_n, sin_b * cos_n + cos_b * sin_n)
        values = flip(block[:, head:])
        for c in range(rows // chunk):
            at = pl.ds(c * chunk, chunk)
            top, mixed = attend(keys, values, c, None)
            top = jnp.where(live, top, -jnp.inf)
            old = tops[:, at]
            diff = top - old
            factor = jnp.exp2(-jnp.abs(diff) * power)
            rises = diff > 0.0
            tops[:, at] = jnp.maximum(old, top)
            total[:, at] = (
                total[:, at] * jnp.where(rises, factor, 1.0)
                + mixed * jnp.where(rises, 1.0, factor))

    peers(lambda d: ask_copy(d, d).wait_recv())
    bring = pltpu.make_async_copy(asks, asks_s, local_sem.at[1])
    asks[me] = request_ref[...]
    bring.start()
    bring.wait()

    def slot_for(d):
        def look(r, slot):
            block_id = asks_s[d, 0, r]
            hit = (block_id // per_device == me) & (r < asks_s[d, 0, requests])
            return jnp.where(hit, lax.rem(block_id, per_device), slot)
        return lax.fori_loop(0, requests, look, jnp.int32(0), unroll=min(requests, 8))

    def reply(first, last):
        def step(s, carry):
            d = lax.rem(me + s * STRIDE, n)
            stage[d] = store[slot_for(d)]
            rare_copy(me, d).start()
            return carry
        lax.fori_loop(first, last, step, 0)

    cuts = [1, 3, 5, WINDOW + 1, n]
    reply(cuts[0], cuts[1])
    recv[me] = store[slot_for(me)]

    for s in range(1, INNER):
        j = lax.rem(inner + s, INNER)
        one_copy(j, j).wait_recv()
    for k in range(pops):
        two_stage[k] = one_recv[lax.rem(pop_ref[k] // per_device, INNER), k]
    for k in range(pops):
        @pl.when(outer != k)
        def _():
            two_copy(outer, k).start()

        @pl.when(outer == k)
        def _():
            two_recv[k] = two_stage[k]

    def rare_fold(h):
        def look(r, found):
            hit = (asks_s[me, 0, r] // per_device == h) & (r < asks_s[me, 0, requests])
            return jnp.where(hit, r, found)
        r = lax.fori_loop(0, requests, look, jnp.int32(-1), unroll=min(requests, 8))
        fold(recv[h], jnp.maximum(r, 0) + 1 + pops, r >= 0)

    def arrivals(first, last):
        def step(s, carry):
            h = lax.rem(me + (n - s) * STRIDE, n)
            rare_copy(h, h).wait_recv()
            rare_fold(h)

            @pl.when(s + WINDOW < n)
            def _():
                reply(s + WINDOW, s + WINDOW + 1)
            return carry
        lax.fori_loop(first, last, step, 0)

    reply(cuts[1], cuts[2])

    own_keys = turn(own_ref[:, :head], own_cos, own_sin)
    own_values = flip(own_ref[:, head:])
    for c in range(rows // chunk):
        at = pl.ds(c * chunk, chunk)
        token = lax.rem(
            lax.broadcasted_iota(jnp.int32, (tokens, chunk), 1) + c * chunk, tokens)
        seen = token >= lax.broadcasted_iota(jnp.int32, (tokens, chunk), 0)
        top, total[:, at] = attend(own_keys, own_values, c, seen)
        tops[:, at] = top

    rare_fold(me)

    @pl.when(outer < pops)
    def _():
        def two_wait(s, carry):
            d = lax.rem(outer + s, outers)
            pltpu.make_async_remote_copy(
                src_ref=mid_stage, dst_ref=two_recv.at[d],
                send_sem=mid_send.at[d], recv_sem=two_sem.at[d],
                device_id={"store": d * INNER + inner}, device_id_type=MESH).wait_recv()
            return carry
        lax.fori_loop(1, outers, two_wait, 0)
        mine = lax.rem(outer, pops)
        mid_stage[...] = two_recv[pop_ref[mine] // (per_device * INNER)]

        def mid_start(s, carry):
            mid_copy(mine, lax.rem(outer + s, outers)).start()
            return carry
        lax.fori_loop(1, outers, mid_start, 0)
        three_stage[mine] = mid_stage[...]

    reply(cuts[2], cuts[3])
    arrivals(cuts[0], cuts[1])
    for k in range(pops):
        @pl.when(outer != k)
        def _():
            mid_copy(k, k).wait_recv()
    for s in range(1, INNER):
        three_copy(inner, lax.rem(inner + s, INNER)).start()
    for k in range(pops):
        popular[inner, k] = three_stage[k]
    arrivals(cuts[1], cuts[3])

    for s in range(1, INNER):
        j = lax.rem(inner + s, INNER)
        three_copy(j, j).wait_recv()

    def popular_fold(k, carry):
        block = jnp.concatenate([popular[j, k] for j in range(INNER)], axis=0)
        fold(block, k + 1, True)
        return carry
    lax.fori_loop(0, pops, popular_fold, 0)

    arrivals(cuts[3], cuts[4])

    for g in range(rows // tokens):
        at = pl.ds(g * tokens, tokens)
        out_ref[:, g * head:(g + 1) * head] = (
            total[:head, at] / total[head:head + 1, at]).T.astype(jnp.bfloat16)

    peers(lambda d: ask_copy(d, d).wait_send())
    peers(lambda d: rare_copy(d, d).wait_send())
    for s in range(1, INNER):
        j = lax.rem(inner + s, INNER)
        one_copy(j, j).wait_send()
        three_copy(j, j).wait_send()

    for k in range(pops):
        @pl.when(outer != k)
        def _():
            two_copy(k, k).wait_send()

    @pl.when(outer < pops)
    def _():
        def mid_done(s, carry):
            d = lax.rem(outer + s, outers)
            mid_copy(lax.rem(outer, pops), d).wait_send()
            return carry
        lax.fori_loop(1, outers, mid_done, 0)


def body(queries, own_kv, store_kv, q_start, pop_ids, pop_pos, rare_ids, rare_count, rare_pos):
    n = lax.axis_size("store")
    tokens = queries.shape[0]
    head = own_kv.shape[1] // 2
    rows = tokens * (queries.shape[1] // head)
    per_device, span, width = store_kv.shape
    requests = rare_ids.shape[1]
    pops = pop_ids.shape[0]
    longest = max(span, tokens)
    lanes = -(-(requests + 1) // 128) * 128
    outers = n // INNER
    piece = span // INNER

    half = np.arange(head) % (head // 2)
    freq = 500000.0 ** (-(2.0 * half) / head)
    sign = np.where(np.arange(head) < head // 2, -1.0, 1.0)
    steps = np.arange(longest)[:, None] * freq[None, :]
    step_cos = np.cos(steps).astype(np.float32)
    step_sin = (np.sin(steps) * sign).astype(np.float32)
    base = jnp.concatenate([q_start, pop_pos[0], rare_pos[0]]).astype(jnp.float32)
    angles = base[:, None] * freq.astype(np.float32)[None, :]
    base_cos = jnp.cos(angles)
    base_sin = jnp.sin(angles) * sign.astype(np.float32)[None, :]
    table = jnp.concatenate([rare_ids[0], rare_count])
    table = jnp.pad(table, (0, lanes - requests - 1))

    vmem = pl.BlockSpec(memory_space=pltpu.VMEM)
    smem = pl.BlockSpec(memory_space=pltpu.SMEM)
    dma = pltpu.SemaphoreType.DMA
    bf16 = jnp.bfloat16
    chunk = min(rows, 256)
    return pl.pallas_call(
        functools.partial(kernel, n, per_device, requests, pops, chunk, head ** -0.5 * np.log2(np.e).item()),
        out_shape=jax.ShapeDtypeStruct(queries.shape, bf16),
        in_specs=[smem, vmem, vmem, vmem, pl.BlockSpec(memory_space=pl.ANY)] + [vmem] * 4,
        out_specs=vmem,
        scratch_shapes=[
            pltpu.VMEM((per_device, span, width), bf16),
            pltpu.VMEM((n, 1, lanes), jnp.int32),
            pltpu.SMEM((n, 1, lanes), jnp.int32),
            pltpu.VMEM((n, span, width), bf16),
            pltpu.VMEM((n, span, width), bf16),
            pltpu.VMEM((rows, head), bf16),
            pltpu.VMEM((head + 16, rows), jnp.float32),
            pltpu.VMEM((1, rows), jnp.float32),
            pltpu.VMEM((INNER, pops, piece, width), bf16),
            pltpu.VMEM((INNER, pops, piece, width), bf16),
            pltpu.VMEM((pops, piece, width), bf16),
            pltpu.VMEM((outers, piece, width), bf16),
            pltpu.VMEM((piece, width), bf16),
            pltpu.VMEM((pops, piece, width), bf16),
            pltpu.VMEM((INNER, pops, piece, width), bf16),
            dma((2,)), dma((n,)), dma((n,)), dma((n,)), dma((n,)),
            dma((INNER,)), dma((INNER,)), dma((outers,)), dma((outers,)), dma((outers,)), dma((pops,)),
            dma((INNER,)), dma((INNER,)),
        ],
        compiler_params=pltpu.CompilerParams(
            collective_id=0, has_side_effects=True, vmem_limit_bytes=60 * 2**20),
    )(pop_ids, table.reshape(1, lanes), queries, own_kv, store_kv,
      base_cos, base_sin, step_cos, step_sin)


def solution(mesh):
    both = ("tenant", "store")
    in_specs = (
        P(both, None), P(both, None), P(both, None, None), P(both), P("tenant"),
        P(both, None), P(both, None), P(both), P(both, None),
    )
    return jax.shard_map(
        body, mesh=mesh, in_specs=in_specs, out_specs=P(both, None), check_vma=False)
```

```python
import functools

import jax
import jax.numpy as jnp
import numpy as np
from jax import lax
from jax.experimental import pallas as pl
from jax.experimental.pallas import tpu as pltpu
from jax.sharding import PartitionSpec as P

MESH = pl.DeviceIdType.MESH
INNER = 4
STRIDE = 5
WINDOW = 7


def kernel(
    n, per_device, requests, pops, chunk, power,
    pop_ref, request_ref, queries_ref, own_ref, store_hbm,
    base_cos, base_sin, step_cos, step_sin, out_ref,
    store, asks, asks_s, stage, recv, query_rows, total, tops,
    one_stage, one_recv, two_stage, two_recv, mid_stage, three_stage, popular,
    local_sem, ask_send, ask_recv, rare_send, rare_recv,
    one_send, one_sem, two_send, two_sem, mid_send, mid_sem, three_send, three_sem,
):
    me = lax.axis_index("store")
    inner, outer = lax.rem(me, INNER), me // INNER
    outers = n // INNER
    head = base_cos.shape[1]
    tokens = queries_ref.shape[0]
    rows = query_rows.shape[0]
    span = stage.shape[1]
    piece = span // INNER

    def ask_copy(slot, target):
        return pltpu.make_async_remote_copy(
            src_ref=request_ref, dst_ref=asks.at[slot],
            send_sem=ask_send.at[target], recv_sem=ask_recv.at[slot],
            device_id={"store": target}, device_id_type=MESH)

    def rare_copy(slot, target):
        return pltpu.make_async_remote_copy(
            src_ref=stage.at[target], dst_ref=recv.at[slot],
            send_sem=rare_send.at[target], recv_sem=rare_recv.at[slot],
            device_id={"store": target}, device_id_type=MESH)

    def one_copy(slot, target):
        return pltpu.make_async_remote_copy(
            src_ref=one_stage.at[target], dst_ref=one_recv.at[slot],
            send_sem=one_send.at[target], recv_sem=one_sem.at[slot],
            device_id={"store": outer * INNER + target}, device_id_type=MESH)

    def two_copy(slot, target):
        return pltpu.make_async_remote_copy(
            src_ref=two_stage.at[target], dst_ref=two_recv.at[slot],
            send_sem=two_send.at[target], recv_sem=two_sem.at[slot],
            device_id={"store": target * INNER + inner}, device_id_type=MESH)

    def mid_copy(slot, target):
        return pltpu.make_async_remote_copy(
            src_ref=mid_stage, dst_ref=three_stage.at[slot],
            send_sem=mid_send.at[target], recv_sem=mid_sem.at[slot],
            device_id={"store": target * INNER + inner}, device_id_type=MESH)

    def three_copy(slot, target):
        return pltpu.make_async_remote_copy(
            src_ref=three_stage, dst_ref=popular.at[slot],
            send_sem=three_send.at[target], recv_sem=three_sem.at[slot],
            device_id={"store": outer * INNER + target}, device_id_type=MESH)

    def peers(act):
        def step(s, carry):
            act(lax.rem(me + s, n))
            return carry
        lax.fori_loop(1, n, step, 0)

    load = pltpu.make_async_copy(store_hbm, store, local_sem.at[0])
    load.start()
    barrier = pltpu.get_barrier_semaphore()
    peers(lambda d: pl.semaphore_signal(
        barrier, inc=1, device_id={"store": d}, device_id_type=MESH))
    pl.semaphore_wait(barrier, n - 1)
    peers(lambda d: ask_copy(me, d).start())
    load.wait()

    for s in range(INNER):
        j = lax.rem(inner + s, INNER)
        begin = pl.multiple_of(j * piece, piece)
        for k in range(pops):
            part = store[lax.rem(pop_ref[k], per_device), pl.ds(begin, piece), :]
            if s == 0:
                one_recv[inner, k] = part
            else:
                one_stage[j, k] = part
        if s:
            one_copy(inner, j).start()

    cos0, sin0 = base_cos[0:1, :], base_sin[0:1, :]
    cos_n, sin_n = step_cos[:tokens, :], step_sin[:tokens, :]
    own_cos = cos0 * cos_n - sin0 * sin_n
    own_sin = sin0 * cos_n + cos0 * sin_n

    def turn(x, cosine, sine):
        x = x.astype(jnp.float32)
        return (x * cosine + pltpu.roll(x, head // 2, 1) * sine).astype(jnp.bfloat16)

    for g in range(rows // tokens):
        query_rows[g * tokens:(g + 1) * tokens, :] = turn(
            queries_ref[:, g * head:(g + 1) * head], own_cos, own_sin)

    pad = total.shape[0] - head

    def attend(keys, values, c, seen):
        at = pl.ds(c * chunk, chunk)
        scores = lax.dot_general(
            keys, query_rows[at, :], (((1,), (1,)), ((), ())),
            preferred_element_type=jnp.float32)
        if seen is not None:
            scores = jnp.where(seen, scores, -jnp.inf)
        top = jnp.max(scores, axis=0, keepdims=True)
        weights = jnp.exp2((scores - top) * power).astype(jnp.bfloat16)
        return top, jnp.dot(values, weights, preferred_element_type=jnp.float32)

    def flip(values):
        return jnp.concatenate(
            [values.T, jnp.ones((pad, values.shape[0]), jnp.bfloat16)], axis=0)

    def fold(block, base, live):
        cos_b, sin_b = base_cos[pl.ds(base, 1), :], base_sin[pl.ds(base, 1), :]
        cos_n, sin_n = step_cos[:span, :], step_sin[:span, :]
        keys = turn(
            block[:, :head], cos_b * cos_n - sin_b * sin_n, sin_b * cos_n + cos_b * sin_n)
        values = flip(block[:, head:])
        for c in range(rows // chunk):
            at = pl.ds(c * chunk, chunk)
            top, mixed = attend(keys, values, c, None)
            top = jnp.where(live, top, -jnp.inf)
            old = tops[:, at]
            diff = top - old
            factor = jnp.exp2(-jnp.abs(diff) * power)
            rises = diff > 0.0
            tops[:, at] = jnp.maximum(old, top)
            total[:, at] = (
                total[:, at] * jnp.where(rises, factor, 1.0)
                + mixed * jnp.where(rises, 1.0, factor))

    peers(lambda d: ask_copy(d, d).wait_recv())
    bring = pltpu.make_async_copy(asks, asks_s, local_sem.at[1])
    asks[me] = request_ref[...]
    bring.start()
    bring.wait()

    def slot_for(d):
        def look(r, slot):
            block_id = asks_s[d, 0, r]
            hit = (block_id // per_device == me) & (r < asks_s[d, 0, requests])
            return jnp.where(hit, lax.rem(block_id, per_device), slot)
        return lax.fori_loop(0, requests, look, jnp.int32(0), unroll=min(requests, 8))

    def reply(first, last):
        def step(s, carry):
            d = lax.rem(me + s * STRIDE, n)
            stage[d] = store[slot_for(d)]
            rare_copy(me, d).start()
            return carry
        lax.fori_loop(first, last, step, 0)

    cuts = [1, 3, 5, WINDOW + 1, n]
    reply(cuts[0], cuts[1])
    recv[me] = store[slot_for(me)]

    for s in range(1, INNER):
        j = lax.rem(inner + s, INNER)
        one_copy(j, j).wait_recv()
    for k in range(pops):
        two_stage[k] = one_recv[lax.rem(pop_ref[k] // per_device, INNER), k]
    for k in range(pops):
        @pl.when(outer != k)
        def _():
            two_copy(outer, k).start()

        @pl.when(outer == k)
        def _():
            two_recv[k] = two_stage[k]

    def rare_fold(h):
        def look(r, found):
            hit = (asks_s[me, 0, r] // per_device == h) & (r < asks_s[me, 0, requests])
            return jnp.where(hit, r, found)
        r = lax.fori_loop(0, requests, look, jnp.int32(-1), unroll=min(requests, 8))
        fold(recv[h], jnp.maximum(r, 0) + 1 + pops, r >= 0)

    def arrivals(first, last):
        def step(s, carry):
            h = lax.rem(me + (n - s) * STRIDE, n)
            rare_copy(h, h).wait_recv()
            rare_fold(h)

            @pl.when(s + WINDOW < n)
            def _():
                reply(s + WINDOW, s + WINDOW + 1)
            return carry
        lax.fori_loop(first, last, step, 0)

    reply(cuts[1], cuts[2])

    own_keys = turn(own_ref[:, :head], own_cos, own_sin)
    own_values = flip(own_ref[:, head:])
    for c in range(rows // chunk):
        at = pl.ds(c * chunk, chunk)
        token = lax.rem(
            lax.broadcasted_iota(jnp.int32, (tokens, chunk), 1) + c * chunk, tokens)
        seen = token >= lax.broadcasted_iota(jnp.int32, (tokens, chunk), 0)
        top, total[:, at] = attend(own_keys, own_values, c, seen)
        tops[:, at] = top

    rare_fold(me)

    @pl.when(outer < pops)
    def _():
        def two_wait(s, carry):
            d = lax.rem(outer + s, outers)
            pltpu.make_async_remote_copy(
                src_ref=mid_stage, dst_ref=two_recv.at[d],
                send_sem=mid_send.at[d], recv_sem=two_sem.at[d],
                device_id={"store": d * INNER + inner}, device_id_type=MESH).wait_recv()
            return carry
        lax.fori_loop(1, outers, two_wait, 0)
        mine = lax.rem(outer, pops)
        mid_stage[...] = two_recv[pop_ref[mine] // (per_device * INNER)]

        def mid_start(s, carry):
            mid_copy(mine, lax.rem(outer + s, outers)).start()
            return carry
        lax.fori_loop(1, outers, mid_start, 0)
        three_stage[mine] = mid_stage[...]

    reply(cuts[2], cuts[3])
    arrivals(cuts[0], cuts[1])
    for k in range(pops):
        @pl.when(outer != k)
        def _():
            mid_copy(k, k).wait_recv()
    for s in range(1, INNER):
        three_copy(inner, lax.rem(inner + s, INNER)).start()
    for k in range(pops):
        popular[inner, k] = three_stage[k]
    arrivals(cuts[1], cuts[3])

    for s in range(1, INNER):
        j = lax.rem(inner + s, INNER)
        three_copy(j, j).wait_recv()

    def popular_fold(k, carry):
        block = jnp.concatenate([popular[j, k] for j in range(INNER)], axis=0)
        fold(block, k + 1, True)
        return carry
    lax.fori_loop(0, pops, popular_fold, 0)

    arrivals(cuts[3], cuts[4])

    for g in range(rows // tokens):
        at = pl.ds(g * tokens, tokens)
        out_ref[:, g * head:(g + 1) * head] = (
            total[:head, at] / total[head:head + 1, at]).T.astype(jnp.bfloat16)

    peers(lambda d: ask_copy(d, d).wait_send())
    peers(lambda d: rare_copy(d, d).wait_send())
    for s in range(1, INNER):
        j = lax.rem(inner + s, INNER)
        one_copy(j, j).wait_send()
        three_copy(j, j).wait_send()

    for k in range(pops):
        @pl.when(outer != k)
        def _():
            two_copy(k, k).wait_send()

    @pl.when(outer < pops)
    def _():
        def mid_done(s, carry):
            d = lax.rem(outer + s, outers)
            mid_copy(lax.rem(outer, pops), d).wait_send()
            return carry
        lax.fori_loop(1, outers, mid_done, 0)


def body(queries, own_kv, store_kv, q_start, pop_ids, pop_pos, rare_ids, rare_count, rare_pos):
    n = lax.axis_size("store")
    tokens = queries.shape[0]
    head = own_kv.shape[1] // 2
    rows = tokens * (queries.shape[1] // head)
    per_device, span, width = store_kv.shape
    requests = rare_ids.shape[1]
    pops = pop_ids.shape[0]
    longest = max(span, tokens)
    lanes = -(-(requests + 1) // 128) * 128
    outers = n // INNER
    piece = span // INNER

    half = np.arange(head) % (head // 2)
    freq = 500000.0 ** (-(2.0 * half) / head)
    sign = np.where(np.arange(head) < head // 2, -1.0, 1.0)
    steps = np.arange(longest)[:, None] * freq[None, :]
    step_cos = np.cos(steps).astype(np.float32)
    step_sin = (np.sin(steps) * sign).astype(np.float32)
    base = jnp.concatenate([q_start, pop_pos[0], rare_pos[0]]).astype(jnp.float32)
    angles = base[:, None] * freq.astype(np.float32)[None, :]
    base_cos = jnp.cos(angles)
    base_sin = jnp.sin(angles) * sign.astype(np.float32)[None, :]
    table = jnp.concatenate([rare_ids[0], rare_count])
    table = jnp.pad(table, (0, lanes - requests - 1))

    vmem = pl.BlockSpec(memory_space=pltpu.VMEM)
    smem = pl.BlockSpec(memory_space=pltpu.SMEM)
    dma = pltpu.SemaphoreType.DMA
    bf16 = jnp.bfloat16
    chunk = min(rows, 512)
    return pl.pallas_call(
        functools.partial(kernel, n, per_device, requests, pops, chunk, head ** -0.5 * np.log2(np.e).item()),
        out_shape=jax.ShapeDtypeStruct(queries.shape, bf16),
        in_specs=[smem, vmem, vmem, vmem, pl.BlockSpec(memory_space=pl.ANY)] + [vmem] * 4,
        out_specs=vmem,
        scratch_shapes=[
            pltpu.VMEM((per_device, span, width), bf16),
            pltpu.VMEM((n, 1, lanes), jnp.int32),
            pltpu.SMEM((n, 1, lanes), jnp.int32),
            pltpu.VMEM((n, span, width), bf16),
            pltpu.VMEM((n, span, width), bf16),
            pltpu.VMEM((rows, head), bf16),
            pltpu.VMEM((head + 16, rows), jnp.float32),
            pltpu.VMEM((1, rows), jnp.float32),
            pltpu.VMEM((INNER, pops, piece, width), bf16),
            pltpu.VMEM((INNER, pops, piece, width), bf16),
            pltpu.VMEM((pops, piece, width), bf16),
            pltpu.VMEM((outers, piece, width), bf16),
            pltpu.VMEM((piece, width), bf16),
            pltpu.VMEM((pops, piece, width), bf16),
            pltpu.VMEM((INNER, pops, piece, width), bf16),
            dma((2,)), dma((n,)), dma((n,)), dma((n,)), dma((n,)),
            dma((INNER,)), dma((INNER,)), dma((outers,)), dma((outers,)), dma((outers,)), dma((pops,)),
            dma((INNER,)), dma((INNER,)),
        ],
        compiler_params=pltpu.CompilerParams(
            collective_id=0, has_side_effects=True, vmem_limit_bytes=60 * 2**20),
    )(pop_ids, table.reshape(1, lanes), queries, own_kv, store_kv,
      base_cos, base_sin, step_cos, step_sin)


def solution(mesh):
    both = ("tenant", "store")
    in_specs = (
        P(both, None), P(both, None), P(both, None, None), P(both), P("tenant"),
        P(both, None), P(both, None), P(both), P(both, None),
    )
    return jax.shard_map(
        body, mesh=mesh, in_specs=in_specs, out_specs=P(both, None), check_vma=False)
```
